32 devices in a mesh: seq: 8 (over z, x), chan: 4 (over y, core).
Axes of the slice: x: 2, y: 2, z: 4, core: 2. Of those that a mesh axis runs over, the one named last changes fastest.
Arguments:
- projected: bfloat16 [1024, 3, 2048], P('seq', None, 'chan'), may hold values from -6 to 6
- short_filter: bfloat16 [3, 16, 3], P(None, 'chan'), may hold values from -3.5 to 3.5
- long_filter: bfloat16 [16, 768], P('chan', 'seq'), may hold values from -0.21875 to 0.21875
- out_weight: bfloat16 [2048, 2048], P('chan'), may hold values from -0.125 to 0.125
Outputs:
- mixer_out: bfloat16 [1024, 2048], P(('seq', 'chan'))
The draws below stay inside these ranges and needn't reach their ends.
All inputs are finite; a program needn't handle non-finite values.
Results may differ from the reference program's by a relative error of at most 0.0057.
Values may be sent and summed in bfloat16 or wider, within the bound.
No kernel may reach another device: no remote copies, remote signals or barrier semaphores. Data moves between devices by JAX's collectives and lax.ppermute only.
A program may use at most 64 MiB of HBM per device.

```python
import jax
import jax.numpy as jnp
from jax import lax

CW = 2048
OUTW = 2048
GSZ = 128
TAPS = 3
FLEN = 768
SG = 16
SEQLEN = 1024


def block_scale(own_key, shape, shards, smallest, top_value):
    def one(dim, parts):
        heights = jax.random.uniform(jax.random.fold_in(jax.random.fold_in(own_key, 6), dim), (parts,), jnp.float32, smallest / len(shards), top_value / len(shards))
        return jnp.repeat(jnp.exp(heights), shape[dim] // parts).reshape((-1,) + (1,) * (len(shape) - dim - 1))

    loudness = one(*shards[0])
    for cut in shards[1:]:
        loudness = loudness * one(*cut)
    return loudness


def scatter_about(rng, extent, spread, most, cuts=(), kind=jnp.bfloat16):
    result = spread * jax.random.normal(rng, extent, jnp.float32)
    if cuts:
        result = result * block_scale(rng, extent, cuts, -0.22, 0.18)
    return jnp.clip(result, -most, most).astype(kind)


def setup_inputs(seed: int = 0) -> dict:
    key_of = jax.random.split(jax.random.key(seed), 5)
    return {
        "projected": scatter_about(key_of[0], (SEQLEN, 3, CW), 1.0, 6.0, ((0, 8), (2, 4))),
        "short_filter": scatter_about(key_of[1], (3, SG, TAPS), TAPS ** -0.5, 3.5, ((1, 4),)),
        "long_filter": scatter_about(key_of[2], (SG, FLEN), FLEN ** -0.5, 0.21875, ((0, 4), (1, 8))),
        "out_weight": scatter_about(key_of[3], (CW, OUTW), CW ** -0.5, 0.125, ((0, 4),)),
    }


def causal_filter(signal, filter_taps, span, seq_len):
    fft_size = seq_len + span
    spectrum = jnp.fft.rfft(signal, n=fft_size, axis=0) * jnp.fft.rfft(filter_taps, n=fft_size)[:, None]
    return jnp.fft.irfft(spectrum, n=fft_size, axis=0)[:seq_len]


def short_causal(signal, filter_taps, seq_len):
    total = jnp.zeros(signal.shape, jnp.float32)
    for lag in range(TAPS):
        moved = jnp.concatenate([jnp.zeros((lag,) + signal.shape[1:], jnp.float32), signal[:seq_len - lag]], axis=0)
        total = total + filter_taps[lag] * moved
    return total


def reference(projected, short_filter, long_filter, out_weight):
    seq_len = projected.shape[0]
    group_count = CW // GSZ
    stacked = projected.reshape(seq_len, 3, group_count, GSZ)

    def one_group(group_index):
        group_block = lax.dynamic_index_in_dim(stacked, group_index, 2, keepdims=False).astype(jnp.float32)
        short_taps = lax.dynamic_index_in_dim(short_filter, group_index, 1, keepdims=False).astype(jnp.float32)
        long_taps = lax.dynamic_index_in_dim(long_filter, group_index, 0, keepdims=False).astype(jnp.float32)
        query_part = short_causal(group_block[:, 0], short_taps[0], seq_len)
        key_part = short_causal(group_block[:, 1], short_taps[1], seq_len)
        value_part = short_causal(group_block[:, 2], short_taps[2], seq_len)
        gated_input = (key_part * value_part).astype(jnp.bfloat16)
        long_out = causal_filter(gated_input.astype(jnp.float32), long_taps, FLEN, seq_len)
        return (query_part * long_out).astype(jnp.bfloat16)

    pieces = lax.map(one_group, jnp.arange(group_count, dtype=jnp.int32))
    gated_all = jnp.transpose(pieces, (1, 0, 2)).reshape(seq_len, CW)
    return jnp.dot(gated_all, out_weight, preferred_element_type=jnp.float32).astype(jnp.bfloat16)
```

```python
import functools

import jax
import jax.numpy as jnp
from jax import lax
from jax.experimental import pallas as pl
from jax.experimental.pallas import tpu as pltpu
from jax.sharding import PartitionSpec as P

REACH = 6
EXTRA = 16


def shifted(array, axis, by):
    peers = lax.axis_size(axis)
    pairs = [(i, i + by) for i in range(peers) if 0 <= i + by < peers]
    return lax.ppermute(array, axis, pairs)


def toeplitz_block(padded, offset, row_count):
    group_count = padded.shape[0]
    window = lax.slice_in_dim(
        padded, offset * row_count + 1, offset * row_count + 2 * row_count, axis=1
    )
    tiled_rows = jnp.tile(window, (1, row_count + 1))[:, : 2 * row_count * row_count]
    tiled_rows = tiled_rows.reshape(group_count, row_count, 2 * row_count)
    return tiled_rows[:, :, :row_count][:, :, ::-1]


def ring_form(projected, short_filter, long_filter, out_weight):
    row_count, _, chan_count = projected.shape
    tap_count = short_filter.shape[-1]
    group_count = short_filter.shape[1]
    group_width = chan_count // group_count
    tail_rows = projected[row_count - tap_count + 1 :]
    arrived_rim = shifted(tail_rows, "seq", 1)
    padded_rows = jnp.concatenate([arrived_rim, projected], axis=0)
    channel_taps = jnp.repeat(short_filter.astype(jnp.float32), group_width, axis=1)
    streams = jnp.zeros((row_count, 3, chan_count), jnp.float32)
    for lag in range(tap_count):
        begin = tap_count - 1 - lag
        window = lax.slice_in_dim(padded_rows, begin, begin + row_count, axis=0)
        streams = streams + channel_taps[None, :, :, lag] * window.astype(jnp.float32)
    query_part = streams[:, 0]
    gated_input = (streams[:, 1] * streams[:, 2]).astype(jnp.bfloat16)
    filters = lax.all_gather(long_filter, "seq", axis=1, tiled=True)
    padded = jnp.pad(filters, ((0, 0), (row_count, row_count)))

    def add_offset(running, offset, source_block):
        matrix = toeplitz_block(padded, offset, row_count)
        shaped_block = source_block.reshape(row_count, group_count, group_width)
        return running + jnp.einsum(
            "gij,jgc->igc", matrix, shaped_block, preferred_element_type=jnp.float32
        )

    running = add_offset(
        jnp.zeros((row_count, group_count, group_width), jnp.float32), 0, gated_input
    )
    moving = gated_input
    for offset in range(1, REACH + 1):
        moving = shifted(moving, "seq", 1)
        running = add_offset(running, offset, moving)
    mixed_out = (query_part * running.reshape(row_count, chan_count)).astype(jnp.bfloat16)
    result = lax.psum_scatter(
        jnp.dot(mixed_out, out_weight, preferred_element_type=jnp.float32),
        "chan",
        scatter_dimension=0,
        tiled=True,
    )
    return result.astype(jnp.bfloat16)


def lagged(stream, lag):
    moved = pltpu.roll(stream, lag, axis=0)
    rows = lax.broadcasted_iota(jnp.int32, stream.shape, 0)
    return jnp.where(rows >= lag, moved, 0.0)


def gate_kernel(copies, proj_ref, short_ref, long_ref, out_ref, extra_ref):
    _, row_count, _ = proj_ref.shape
    group_count = short_ref.shape[1]
    width = proj_ref.shape[2] // group_count
    lags = long_ref.shape[1]
    taps = [short_ref[s].astype(jnp.float32) for s in range(3)]
    long_rows = long_ref[...].astype(jnp.float32)
    extra_ref[...] = jnp.zeros_like(extra_ref)
    for g in range(group_count):
        lanes = slice(g * width, (g + 1) * width)
        raw = [proj_ref[s, :, lanes].astype(jnp.float32) for s in range(3)]
        made = []
        for s in (1, 2):
            tap = [taps[s][g : g + 1, m : m + 1] for m in range(3)]
            made.append(
                tap[0] * raw[s] + tap[1] * lagged(raw[s], 1) + tap[2] * lagged(raw[s], 2)
            )
        gated = (made[0] * made[1]).astype(jnp.bfloat16)
        extra_ref[g, 0:1, 0:lags] = long_rows[g : g + 1]
        extra_ref[g, 1:3] = raw[1][0:2]
        extra_ref[g, 3:5] = raw[2][0:2]
        extra_ref[g, 5:7] = raw[1][row_count - 2 :]
        extra_ref[g, 7:9] = raw[2][row_count - 2 :]
        extra_ref[g, 9:11] = raw[0][row_count - 2 :]
        extra = extra_ref[g].astype(jnp.bfloat16)
        for x in range(copies):
            out_ref[g * copies + x, 0:row_count] = gated
            out_ref[g * copies + x, row_count:] = extra


def filter_kernel(copies, lags, place_ref, in_ref, short_ref, out_ref, gated_ref):
    seq_count, rows_sent, width = in_ref.shape
    row_count = rows_sent - EXTRA
    depth = REACH * row_count
    me = place_ref[0]
    group, part = me // copies, me % copies

    picked = []
    for s in (1, 2):
        table = short_ref[s].astype(jnp.float32)
        rows = lax.broadcasted_iota(jnp.int32, table.shape, 0)
        row = jnp.sum(jnp.where(rows == group, table, 0.0), axis=0, keepdims=True)
        picked.append([row[:, m : m + 1] for m in range(3)])

    gated_ref[0:depth] = jnp.zeros((depth, width), jnp.bfloat16)
    tile_rows = lax.broadcasted_iota(jnp.int32, (16, width), 0)
    before = jnp.zeros((EXTRA, width), jnp.float32)
    lag_rows = []
    for s in range(seq_count):
        here = in_ref[s, row_count:].astype(jnp.float32)
        lag_rows.append(here[0:1])
        heads = []
        for stream in range(2):
            tap = picked[stream]
            first, second = here[1 + 2 * stream : 2 + 2 * stream], here[2 + 2 * stream : 3 + 2 * stream]
            older, newer = before[5 + 2 * stream : 6 + 2 * stream], before[6 + 2 * stream : 7 + 2 * stream]
            heads.append(
                (
                    tap[0] * first + tap[1] * newer + tap[2] * older,
                    tap[0] * second + tap[1] * first + tap[2] * newer,
                )
            )
        tile = in_ref[s, 0:16].astype(jnp.float32)
        tile = jnp.where(tile_rows == 0, heads[0][0] * heads[1][0], tile)
        tile = jnp.where(tile_rows == 1, heads[0][1] * heads[1][1], tile)
        base = depth + s * row_count
        gated_ref[base : base + 16] = tile.astype(jnp.bfloat16)
        gated_ref[base + 16 : base + row_count] = in_ref[s, 16:row_count]
        before = here

    lags_back = jnp.concatenate(lag_rows[::-1], axis=0).astype(jnp.bfloat16)
    i = lax.broadcasted_iota(jnp.int32, (width, width), 0)
    k = lax.broadcasted_iota(jnp.int32, (width, width), 1)
    flip = jnp.where(i + k == lags - 1, 1.0, 0.0).astype(jnp.bfloat16)
    turned = jnp.dot(lags_back, flip, preferred_element_type=jnp.float32)
    span = depth + 2 * row_count
    first_lane = depth - lags * seq_count + 1
    blank = jnp.zeros((1, span - width), jnp.float32)
    line = jnp.zeros((1, span), jnp.float32)
    for s in range(seq_count):
        piece = jnp.concatenate([turned[s : s + 1], blank], axis=1)
        line = line + pltpu.roll(piece, first_lane + lags * s, axis=1)
    strip = pltpu.roll(
        jnp.broadcast_to(line, (row_count, span)), 0, axis=1, stride=1, stride_axis=0
    )
    strip = strip[:, : depth + row_count].astype(jnp.bfloat16)

    for z in range(out_ref.shape[0]):
        block = z * copies + part
        start = pl.multiple_of(block * row_count, row_count)
        source = gated_ref[pl.ds(start, depth + row_count), :]
        made = jnp.dot(strip, source, preferred_element_type=jnp.float32)
        out_ref[z, 0:row_count] = made.astype(jnp.bfloat16)
        rim = in_ref[jnp.maximum(block - 1, 0), row_count:].astype(jnp.float32)
        out_ref[z, row_count:] = jnp.where(block > 0, rim, 0.0).astype(jnp.bfloat16)


def project_kernel(place_ref, in_ref, proj_ref, short_ref, weight_ref, send_ref, keep_ref, mixed_ref):
    group_count, rows_sent, width = in_ref.shape
    row_count = rows_sent - EXTRA
    taps = short_ref[0].astype(jnp.float32)
    rows = lax.broadcasted_iota(jnp.int32, (row_count, width), 0)
    for g in range(group_count):
        lanes = slice(g * width, (g + 1) * width)
        query = proj_ref[0, :, lanes].astype(jnp.float32)
        rim = in_ref[g, row_count:].astype(jnp.float32)
        older, newer = rim[9:10], rim[10:11]
        one = jnp.where(rows == 0, newer, pltpu.roll(query, 1, axis=0))
        two = jnp.where(rows == 0, older, jnp.where(rows == 1, newer, pltpu.roll(query, 2, axis=0)))
        tap = [taps[g : g + 1, m : m + 1] for m in range(3)]
        made = tap[0] * query + tap[1] * one + tap[2] * two
        long_out = in_ref[g, 0:row_count].astype(jnp.float32)
        mixed_ref[:, lanes] = (made * long_out).astype(jnp.bfloat16)
    quarter = row_count // 4
    me = place_ref[0]

    def take(member):
        return mixed_ref[pl.ds(pl.multiple_of(member * quarter, quarter), quarter), :]

    ordered = jnp.concatenate([take(me ^ 1), take(me ^ 3), take(me), take(me ^ 2)], axis=0)
    step = 512
    for c in range(0, weight_ref.shape[1], step):
        made = jnp.dot(
            ordered, weight_ref[:, c : c + step], preferred_element_type=jnp.float32
        )
        send_ref[:, c : c + step] = made[: 2 * quarter].astype(jnp.bfloat16)
        keep_ref[:, c : c + step] = made[2 * quarter :]


def whole(space=pltpu.VMEM):
    return pl.BlockSpec(memory_space=space)


def exchange_form(projected, short_filter, long_filter, out_weight):
    row_count, _, chan_count = projected.shape
    group_count = short_filter.shape[1]
    width = chan_count // group_count
    seq_count = lax.axis_size("seq")
    copies = seq_count // group_count
    lags = long_filter.shape[1]
    rows_sent = row_count + EXTRA
    streams = jnp.transpose(projected, (1, 0, 2))
    seq_place = lax.axis_index("seq").astype(jnp.int32).reshape(1)
    chan_place = lax.axis_index("chan").astype(jnp.int32).reshape(1)

    outgoing = pl.pallas_call(
        functools.partial(gate_kernel, copies),
        out_shape=jax.ShapeDtypeStruct((seq_count, rows_sent, width), jnp.bfloat16),
        in_specs=[whole()] * 3,
        out_specs=whole(),
        scratch_shapes=[pltpu.VMEM((group_count, EXTRA, width), jnp.float32)],
        name="gate",
    )(streams, short_filter, long_filter)
    arrived = lax.all_to_all(outgoing, "seq", 0, 0)
    made = pl.pallas_call(
        functools.partial(filter_kernel, copies, lags),
        out_shape=jax.ShapeDtypeStruct((group_count, rows_sent, width), jnp.bfloat16),
        in_specs=[whole(pltpu.SMEM), whole(), whole()],
        out_specs=whole(),
        scratch_shapes=[pltpu.VMEM(((REACH + seq_count) * row_count, width), jnp.bfloat16)],
        name="long_filter",
    )(seq_place, arrived, short_filter)
    same_part = [[z * copies + x for z in range(group_count)] for x in range(copies)]
    returned = lax.all_to_all(made, "seq", 0, 0, axis_index_groups=same_part)
    half = row_count // 2
    send, keep = pl.pallas_call(
        project_kernel,
        out_shape=(
            jax.ShapeDtypeStruct((half, out_weight.shape[1]), jnp.bfloat16),
            jax.ShapeDtypeStruct((half, out_weight.shape[1]), jnp.float32),
        ),
        in_specs=[whole(pltpu.SMEM)] + [whole()] * 4,
        out_specs=(whole(), whole()),
        scratch_shapes=[pltpu.VMEM((row_count, chan_count), jnp.bfloat16)],
        name="project",
    )(chan_place, returned, streams, short_filter, out_weight)
    near = lax.ppermute(send, "chan", [(c, c ^ 1) for c in range(4)])
    quarter = half // 2
    onward = (keep[quarter:] + near[quarter:].astype(jnp.float32)).astype(jnp.bfloat16)
    far = lax.ppermute(onward, "chan", [(c, c ^ 2) for c in range(4)])
    mine = keep[:quarter] + near[:quarter].astype(jnp.float32)
    return (mine + far.astype(jnp.float32)).astype(jnp.bfloat16)


def on_device(projected, short_filter, long_filter, out_weight):
    row_count, _, chan_count = projected.shape
    group_count = short_filter.shape[1]
    width = chan_count // group_count
    seq_count = lax.axis_size("seq")
    exchanged = (seq_count + group_count) * (row_count + EXTRA) * width
    ringed = REACH * row_count * chan_count
    fits = (
        seq_count % group_count == 0
        and seq_count * long_filter.shape[1] <= REACH * row_count
        and long_filter.shape[1] <= width
        and width == 128
        and row_count % 64 == 0
        and short_filter.shape[-1] == 3
        and lax.axis_size("chan") == 4
    )
    form = exchange_form if fits and exchanged < ringed else ring_form
    return form(projected, short_filter, long_filter, out_weight)


def solution(mesh):
    return jax.shard_map(
        on_device,
        mesh=mesh,
        in_specs=(P("seq", None, "chan"), P(None, "chan", None), P("chan", "seq"), P("chan", None)),
        out_specs=P(("seq", "chan"), None),
        check_vma=False,
    )
```

```python
import functools

import jax
import jax.numpy as jnp
from jax import lax
from jax.experimental import pallas as pl
from jax.experimental.pallas import tpu as pltpu
from jax.sharding import PartitionSpec as P

REACH = 6
EXTRA = 8


def shifted(array, axis, by):
    peers = lax.axis_size(axis)
    pairs = [(i, i + by) for i in range(peers) if 0 <= i + by < peers]
    return lax.ppermute(array, axis, pairs)


def toeplitz_block(padded, offset, row_count):
    group_count = padded.shape[0]
    window = lax.slice_in_dim(
        padded, offset * row_count + 1, offset * row_count + 2 * row_count, axis=1
    )
    tiled_rows = jnp.tile(window, (1, row_count + 1))[:, : 2 * row_count * row_count]
    tiled_rows = tiled_rows.reshape(group_count, row_count, 2 * row_count)
    return tiled_rows[:, :, :row_count][:, :, ::-1]


def ring_form(projected, short_filter, long_filter, out_weight):
    row_count, _, chan_count = projected.shape
    tap_count = short_filter.shape[-1]
    group_count = short_filter.shape[1]
    group_width = chan_count // group_count
    tail_rows = projected[row_count - tap_count + 1 :]
    arrived_rim = shifted(tail_rows, "seq", 1)
    padded_rows = jnp.concatenate([arrived_rim, projected], axis=0)
    channel_taps = jnp.repeat(short_filter.astype(jnp.float32), group_width, axis=1)
    streams = jnp.zeros((row_count, 3, chan_count), jnp.float32)
    for lag in range(tap_count):
        begin = tap_count - 1 - lag
        window = lax.slice_in_dim(padded_rows, begin, begin + row_count, axis=0)
        streams = streams + channel_taps[None, :, :, lag] * window.astype(jnp.float32)
    query_part = streams[:, 0]
    gated_input = (streams[:, 1] * streams[:, 2]).astype(jnp.bfloat16)
    filters = lax.all_gather(long_filter, "seq", axis=1, tiled=True)
    padded = jnp.pad(filters, ((0, 0), (row_count, row_count)))

    def add_offset(running, offset, source_block):
        matrix = toeplitz_block(padded, offset, row_count)
        shaped_block = source_block.reshape(row_count, group_count, group_width)
        return running + jnp.einsum(
            "gij,jgc->igc", matrix, shaped_block, preferred_element_type=jnp.float32
        )

    running = add_offset(
        jnp.zeros((row_count, group_count, group_width), jnp.float32), 0, gated_input
    )
    moving = gated_input
    for offset in range(1, REACH + 1):
        moving = shifted(moving, "seq", 1)
        running = add_offset(running, offset, moving)
    mixed_out = (query_part * running.reshape(row_count, chan_count)).astype(jnp.bfloat16)
    result = lax.psum_scatter(
        jnp.dot(mixed_out, out_weight, preferred_element_type=jnp.float32),
        "chan",
        scatter_dimension=0,
        tiled=True,
    )
    return result.astype(jnp.bfloat16)


def lagged(stream, lag):
    moved = pltpu.roll(stream, lag, axis=0)
    rows = lax.broadcasted_iota(jnp.int32, stream.shape, 0)
    return jnp.where(rows >= lag, moved, 0.0)


def short_sum(stream, table, group):
    tap = [table[group : group + 1, m : m + 1] for m in range(3)]
    return tap[0] * stream + tap[1] * lagged(stream, 1) + tap[2] * lagged(stream, 2)


def gate_kernel(copies, proj_hbm, short_hbm, long_hbm, out_hbm, proj_ref, short_ref, long_ref, extra_ref, made_ref, sems, out_sems):
    group_count, _, row_count, width = proj_ref.shape
    lags = long_ref.shape[1]
    small = [
        pltpu.make_async_copy(short_hbm, short_ref, sems.at[0]),
        pltpu.make_async_copy(long_hbm, long_ref, sems.at[1]),
    ]
    large = [
        pltpu.make_async_copy(
            proj_hbm.at[1:3, :, g * width : (g + 1) * width], proj_ref.at[g], sems.at[2 + g]
        )
        for g in range(group_count)
    ]
    for copy in small + large:
        copy.start()
    extra_ref[...] = jnp.zeros_like(extra_ref)
    for copy in small:
        copy.wait()
    tables = [short_ref[s].astype(jnp.float32) for s in (1, 2)]
    long_rows = long_ref[...].astype(jnp.float32)
    leaving = []
    for g in range(group_count):
        large[g].wait()
        key, value = (proj_ref[g, s].astype(jnp.float32) for s in range(2))
        gated = short_sum(key, tables[0], g) * short_sum(value, tables[1], g)
        rows = lax.broadcasted_iota(jnp.int32, gated.shape, 0)
        extra_ref[g, 0:1, 0:lags] = long_rows[g : g + 1]
        extra_ref[g, 1:3] = value[0:2]
        extra_ref[g, 3:5] = key[row_count - 2 :]
        extra_ref[g, 5:7] = value[row_count - 2 :]
        made_ref[g, 0:row_count] = jnp.where(rows < 2, key, gated).astype(jnp.bfloat16)
        made_ref[g, row_count:] = extra_ref[g].astype(jnp.bfloat16)
        for x in range(copies):
            member = g * copies + x
            copy = pltpu.make_async_copy(made_ref.at[g], out_hbm.at[member], out_sems.at[member])
            copy.start()
            leaving.append(copy)
    for copy in leaving:
        copy.wait()


def ready_kernel(proj_hbm, short_hbm, weight_hbm, query_ref, table_ref, weight_ref, proj_ref, short_ref, sems):
    copies = [
        pltpu.make_async_copy(short_hbm, short_ref, sems.at[0]),
        pltpu.make_async_copy(proj_hbm.at[0], proj_ref, sems.at[1]),
        pltpu.make_async_copy(weight_hbm, weight_ref, sems.at[2]),
    ]
    for copy in copies:
        copy.start()
    copies[0].wait()
    for s in range(3):
        table_ref[s] = short_ref[s].astype(jnp.float32)
    table = short_ref[0].astype(jnp.float32)
    group_count = table.shape[0]
    width = query_ref.shape[1] // group_count
    copies[1].wait()
    for g in range(group_count):
        lanes = slice(g * width, (g + 1) * width)
        query_ref[:, lanes] = short_sum(proj_ref[:, lanes].astype(jnp.float32), table, g)
    copies[2].wait()


def filter_kernel(copies, lags, place_ref, in_ref, table_ref, out_hbm, gated_ref, made_ref, sems):
    seq_count, rows_sent, width = in_ref.shape
    row_count = rows_sent - EXTRA
    depth = REACH * row_count
    me = place_ref[0]
    group, part = me // copies, me % copies

    extras = [in_ref[s, row_count:].astype(jnp.float32) for s in range(seq_count)]
    lags_back = jnp.concatenate([e[0:1] for e in extras[::-1]], axis=0).astype(jnp.bfloat16)
    i = lax.broadcasted_iota(jnp.int32, (width, width), 0)
    k = lax.broadcasted_iota(jnp.int32, (width, width), 1)
    flip = jnp.where(i + k == lags - 1, 1.0, 0.0).astype(jnp.bfloat16)
    turned = jnp.dot(lags_back, flip, preferred_element_type=jnp.float32)
    span = depth + 2 * row_count
    first_lane = depth - lags * seq_count + 1
    blank = jnp.zeros((1, span - width), jnp.float32)
    line = jnp.zeros((1, span), jnp.float32)
    for s in range(seq_count):
        piece = jnp.concatenate([turned[s : s + 1], blank], axis=1)
        line = line + pltpu.roll(piece, first_lane + lags * s, axis=1)
    strip = pltpu.roll(
        jnp.broadcast_to(line, (row_count, span)), 0, axis=1, stride=1, stride_axis=0
    )
    strip = strip[:, : depth + row_count].astype(jnp.bfloat16)

    picked = []
    for s in (1, 2):
        table = table_ref[s]
        rows = lax.broadcasted_iota(jnp.int32, table.shape, 0)
        row = jnp.sum(jnp.where(rows == group, table, 0.0), axis=0, keepdims=True)
        picked.append([row[:, m : m + 1] for m in range(3)])

    gated_ref[0:depth] = jnp.zeros((depth, width), jnp.bfloat16)
    tile_rows = lax.broadcasted_iota(jnp.int32, (16, width), 0)
    before = jnp.zeros((EXTRA, width), jnp.float32)
    for s in range(seq_count):
        here = extras[s]
        tile = in_ref[s, 0:16].astype(jnp.float32)
        heads = []
        for stream, head in enumerate((tile[0:2], here[1:3])):
            tap = picked[stream]
            first, second = head[0:1], head[1:2]
            older, newer = before[3 + 2 * stream : 4 + 2 * stream], before[4 + 2 * stream : 5 + 2 * stream]
            heads.append(
                (
                    tap[0] * first + tap[1] * newer + tap[2] * older,
                    tap[0] * second + tap[1] * first + tap[2] * newer,
                )
            )
        tile = jnp.where(tile_rows == 0, heads[0][0] * heads[1][0], tile)
        tile = jnp.where(tile_rows == 1, heads[0][1] * heads[1][1], tile)
        base = depth + s * row_count
        gated_ref[base : base + 16] = tile.astype(jnp.bfloat16)
        gated_ref[base + 16 : base + row_count] = in_ref[s, 16:row_count]
        before = here

    leaving = []
    for z in range(out_hbm.shape[0]):
        start = pl.multiple_of((z * copies + part) * row_count, row_count)
        source = gated_ref[pl.ds(start, depth + row_count), :]
        made = jnp.dot(strip, source, preferred_element_type=jnp.float32)
        made_ref[z] = made.astype(jnp.bfloat16)
        copy = pltpu.make_async_copy(made_ref.at[z], out_hbm.at[z], sems.at[z])
        copy.start()
        leaving.append(copy)
    for copy in leaving:
        copy.wait()


def project_kernel(place_ref, in_ref, query_ref, rim_ref, table_ref, weight_ref, send_ref, keep_ref, mixed_ref):
    group_count, row_count, width = in_ref.shape
    table = table_ref[0]
    rows = lax.broadcasted_iota(jnp.int32, (8, width), 0)
    rim = rim_ref[...].astype(jnp.float32)
    for g in range(group_count):
        lanes = slice(g * width, (g + 1) * width)
        older, newer = rim[0:1, lanes], rim[1:2, lanes]
        one, two = table[g : g + 1, 1:2], table[g : g + 1, 2:3]
        head = query_ref[0:8, lanes]
        head = head + jnp.where(rows == 0, one * newer + two * older, 0.0)
        head = head + jnp.where(rows == 1, two * newer, 0.0)
        query = jnp.concatenate([head, query_ref[8:, lanes]], axis=0)
        mixed_ref[:, lanes] = (query * in_ref[g].astype(jnp.float32)).astype(jnp.bfloat16)
    quarter = row_count // 4
    me = place_ref[0]

    def take(member):
        return mixed_ref[pl.ds(pl.multiple_of(member * quarter, quarter), quarter), :]

    ordered = jnp.concatenate([take(me ^ 1), take(me ^ 3), take(me), take(me ^ 2)], axis=0)
    step = 512
    for c in range(0, weight_ref.shape[1], step):
        made = jnp.dot(
            ordered, weight_ref[:, c : c + step], preferred_element_type=jnp.float32
        )
        send_ref[:, c : c + step] = made[: 2 * quarter].astype(jnp.bfloat16)
        keep_ref[:, c : c + step] = made[2 * quarter :]


def room(mib):
    return pltpu.CompilerParams(vmem_limit_bytes=mib << 20)


def cost(flops, moved):
    return pl.CostEstimate(flops=flops, bytes_accessed=moved, transcendentals=0)


def whole(space=pltpu.VMEM):
    return pl.BlockSpec(memory_space=space)


def exchange_form(projected, short_filter, long_filter, out_weight):
    row_count, _, chan_count = projected.shape
    group_count = short_filter.shape[1]
    width = chan_count // group_count
    out_count = out_weight.shape[1]
    seq_count = lax.axis_size("seq")
    copies = seq_count // group_count
    lags = long_filter.shape[1]
    rows_sent = row_count + EXTRA
    streams = jnp.transpose(projected, (1, 0, 2))
    seq_place = lax.axis_index("seq").astype(jnp.int32).reshape(1)
    chan_place = lax.axis_index("chan").astype(jnp.int32).reshape(1)
    block_bytes = row_count * chan_count * 2

    outgoing = pl.pallas_call(
        functools.partial(gate_kernel, copies),
        out_shape=jax.ShapeDtypeStruct((seq_count, rows_sent, width), jnp.bfloat16),
        in_specs=[whole(pltpu.HBM)] * 3,
        out_specs=whole(pltpu.HBM),
        scratch_shapes=[
            pltpu.VMEM((group_count, 2, row_count, width), projected.dtype),
            pltpu.VMEM(short_filter.shape, short_filter.dtype),
            pltpu.VMEM(long_filter.shape, long_filter.dtype),
            pltpu.VMEM((group_count, EXTRA, width), jnp.float32),
            pltpu.VMEM((group_count, rows_sent, width), jnp.bfloat16),
            pltpu.SemaphoreType.DMA((2 + group_count,)),
            pltpu.SemaphoreType.DMA((seq_count,)),
        ],
        cost_estimate=cost(12 * row_count * chan_count, 4 * block_bytes),
        name="gate",
    )(streams, short_filter, long_filter)
    arrived = lax.all_to_all(outgoing, "seq", 0, 0)

    query, table, weight = pl.pallas_call(
        ready_kernel,
        out_shape=(
            jax.ShapeDtypeStruct((row_count, chan_count), jnp.float32),
            jax.ShapeDtypeStruct(short_filter.shape, jnp.float32),
            jax.ShapeDtypeStruct(out_weight.shape, out_weight.dtype),
        ),
        in_specs=[whole(pltpu.HBM)] * 3,
        out_specs=(whole(), whole(), whole()),
        scratch_shapes=[
            pltpu.VMEM((row_count, chan_count), projected.dtype),
            pltpu.VMEM(short_filter.shape, short_filter.dtype),
            pltpu.SemaphoreType.DMA((3,)),
        ],
        compiler_params=room(4),
        cost_estimate=cost(6 * row_count * chan_count, 2 * chan_count * out_count + 3 * block_bytes),
        name="ready",
    )(streams, short_filter, out_weight)
    rim = shifted(projected[row_count - 2 :, 0], "seq", 1)

    made = pl.pallas_call(
        functools.partial(filter_kernel, copies, lags),
        out_shape=jax.ShapeDtypeStruct((group_count, row_count, width), jnp.bfloat16),
        in_specs=[whole(pltpu.SMEM), whole(), whole()],
        out_specs=whole(pltpu.HBM),
        scratch_shapes=[
            pltpu.VMEM(((REACH + seq_count) * row_count, width), jnp.bfloat16),
            pltpu.VMEM((group_count, row_count, width), jnp.bfloat16),
            pltpu.SemaphoreType.DMA((group_count,)),
        ],
        compiler_params=room(4),
        cost_estimate=cost(
            2 * group_count * (REACH + 1) * row_count * row_count * width, 4 * block_bytes
        ),
        name="long_filter",
    )(seq_place, arrived, table)
    same_part = [[z * copies + x for z in range(group_count)] for x in range(copies)]
    returned = lax.all_to_all(made, "seq", 0, 0, axis_index_groups=same_part)
    half = row_count // 2
    send, keep = pl.pallas_call(
        project_kernel,
        out_shape=(
            jax.ShapeDtypeStruct((half, out_count), jnp.bfloat16),
            jax.ShapeDtypeStruct((half, out_count), jnp.float32),
        ),
        in_specs=[whole(pltpu.SMEM)] + [whole()] * 5,
        out_specs=(whole(), whole()),
        scratch_shapes=[pltpu.VMEM((row_count, chan_count), jnp.bfloat16)],
        compiler_params=room(4),
        cost_estimate=cost(2 * row_count * chan_count * out_count, 2 * chan_count * out_count),
        name="project",
    )(chan_place, returned, query, rim, table, weight)
    near = lax.ppermute(send, "chan", [(c, c ^ 1) for c in range(4)])
    quarter = half // 2
    onward = (keep[quarter:] + near[quarter:].astype(jnp.float32)).astype(jnp.bfloat16)
    far = lax.ppermute(onward, "chan", [(c, c ^ 2) for c in range(4)])
    mine = keep[:quarter] + near[:quarter].astype(jnp.float32)
    return (mine + far.astype(jnp.float32)).astype(jnp.bfloat16)


def on_device(projected, short_filter, long_filter, out_weight):
    row_count, _, chan_count = projected.shape
    group_count = short_filter.shape[1]
    width = chan_count // group_count
    seq_count = lax.axis_size("seq")
    exchanged = (seq_count + group_count) * (row_count + EXTRA) * width
    ringed = REACH * row_count * chan_count
    fits = (
        seq_count % group_count == 0
        and seq_count * long_filter.shape[1] <= REACH * row_count
        and long_filter.shape[1] <= width
        and width == 128
        and row_count % 64 == 0
        and short_filter.shape[-1] == 3
        and lax.axis_size("chan") == 4
    )
    form = exchange_form if fits and exchanged < ringed else ring_form
    return form(projected, short_filter, long_filter, out_weight)


def solution(mesh):
    return jax.shard_map(
        on_device,
        mesh=mesh,
        in_specs=(P("seq", None, "chan"), P(None, "chan", None), P("chan", "seq"), P("chan", None)),
        out_specs=P(("seq", "chan"), None),
        check_vma=False,
    )
```

```python
import functools

import jax
import jax.numpy as jnp
from jax import lax
from jax.experimental import pallas as pl
from jax.experimental.pallas import tpu as pltpu
from jax.sharding import PartitionSpec as P

REACH = 6
EXTRA = 16
RIM = 8


def shifted(array, axis, by):
    peers = lax.axis_size(axis)
    pairs = [(i, i + by) for i in range(peers) if 0 <= i + by < peers]
    return lax.ppermute(array, axis, pairs)


def toeplitz_block(padded, offset, row_count):
    group_count = padded.shape[0]
    window = lax.slice_in_dim(
        padded, offset * row_count + 1, offset * row_count + 2 * row_count, axis=1
    )
    tiled_rows = jnp.tile(window, (1, row_count + 1))[:, : 2 * row_count * row_count]
    tiled_rows = tiled_rows.reshape(group_count, row_count, 2 * row_count)
    return tiled_rows[:, :, :row_count][:, :, ::-1]


def ring_form(projected, short_filter, long_filter, out_weight):
    row_count, _, chan_count = projected.shape
    tap_count = short_filter.shape[-1]
    group_count = short_filter.shape[1]
    group_width = chan_count // group_count
    tail_rows = projected[row_count - tap_count + 1 :]
    arrived_rim = shifted(tail_rows, "seq", 1)
    padded_rows = jnp.concatenate([arrived_rim, projected], axis=0)
    channel_taps = jnp.repeat(short_filter.astype(jnp.float32), group_width, axis=1)
    streams = jnp.zeros((row_count, 3, chan_count), jnp.float32)
    for lag in range(tap_count):
        begin = tap_count - 1 - lag
        window = lax.slice_in_dim(padded_rows, begin, begin + row_count, axis=0)
        streams = streams + channel_taps[None, :, :, lag] * window.astype(jnp.float32)
    query_part = streams[:, 0]
    gated_input = (streams[:, 1] * streams[:, 2]).astype(jnp.bfloat16)
    filters = lax.all_gather(long_filter, "seq", axis=1, tiled=True)
    padded = jnp.pad(filters, ((0, 0), (row_count, row_count)))

    def add_offset(running, offset, source_block):
        matrix = toeplitz_block(padded, offset, row_count)
        shaped_block = source_block.reshape(row_count, group_count, group_width)
        return running + jnp.einsum(
            "gij,jgc->igc", matrix, shaped_block, preferred_element_type=jnp.float32
        )

    running = add_offset(
        jnp.zeros((row_count, group_count, group_width), jnp.float32), 0, gated_input
    )
    moving = gated_input
    for offset in range(1, REACH + 1):
        moving = shifted(moving, "seq", 1)
        running = add_offset(running, offset, moving)
    mixed_out = (query_part * running.reshape(row_count, chan_count)).astype(jnp.bfloat16)
    result = lax.psum_scatter(
        jnp.dot(mixed_out, out_weight, preferred_element_type=jnp.float32),
        "chan",
        scatter_dimension=0,
        tiled=True,
    )
    return result.astype(jnp.bfloat16)


def lagged(stream, lag):
    moved = pltpu.roll(stream, lag, axis=0)
    rows = lax.broadcasted_iota(jnp.int32, stream.shape, 0)
    return jnp.where(rows >= lag, moved, 0.0)


def taps_of(table, group):
    rows = lax.broadcasted_iota(jnp.int32, table.shape, 0)
    row = jnp.sum(jnp.where(rows == group, table, 0.0), axis=0, keepdims=True)
    return [row[:, m : m + 1] for m in range(3)]


def short_sum(stream, tap):
    return tap[0] * stream + tap[1] * lagged(stream, 1) + tap[2] * lagged(stream, 2)


def gate_kernel(copies, place_ref, proj_hbm, short_hbm, long_hbm, *refs):
    group_count, row_count = long_hbm.shape[0], proj_hbm.shape[1]
    out_refs, table_ref = refs[:group_count], refs[group_count]
    proj_ref, short_ref, long_ref, extra_ref, tail_ref, sems = refs[group_count + 1 :]
    width = proj_ref.shape[-1]
    lags = long_ref.shape[1]
    mine = place_ref[0] // copies
    small = [
        pltpu.make_async_copy(short_hbm, short_ref, sems.at[0]),
        pltpu.make_async_copy(long_hbm, long_ref, sems.at[1]),
        pltpu.make_async_copy(proj_hbm.at[0, row_count - 8 :], tail_ref, sems.at[2]),
    ]
    order = list(range(group_count))[::-1]
    large = {}
    for d in order:
        lanes = pl.ds(pl.multiple_of((mine ^ d) * width, width), width)
        large[d] = pltpu.make_async_copy(proj_hbm.at[1:3, :, lanes], proj_ref.at[d], sems.at[3 + d])
    for copy in small + [large[d] for d in order]:
        copy.start()
    extra_ref[...] = jnp.zeros_like(extra_ref)
    for copy in small:
        copy.wait()
    tables = [short_ref[s].astype(jnp.float32) for s in (1, 2)]
    for s in range(3):
        table_ref[s] = short_ref[s].astype(jnp.float32)
    long_rows = long_ref[...].astype(jnp.float32)
    long_row_ids = lax.broadcasted_iota(jnp.int32, long_rows.shape, 0)
    for d in order:
        group = mine ^ d
        taps = [taps_of(table, group) for table in tables]
        picked = jnp.where(long_row_ids == group, long_rows, 0.0)
        extra_ref[d, 0:1, 0:lags] = jnp.sum(picked, axis=0, keepdims=True)
        large[d].wait()
        key, value = (proj_ref[d, s].astype(jnp.float32) for s in range(2))
        gated = short_sum(key, taps[0]) * short_sum(value, taps[1])
        rows = lax.broadcasted_iota(jnp.int32, gated.shape, 0)
        extra_ref[d, 1:3] = value[0:2]
        extra_ref[d, 3:5] = key[row_count - 2 :]
        extra_ref[d, 5:7] = value[row_count - 2 :]
        lanes = pl.ds(pl.multiple_of(group * width, width), width)
        extra_ref[d, 8:10] = tail_ref[:, lanes].astype(jnp.float32)[6:8]
        out_refs[d][0:row_count] = jnp.where(rows < 2, key, gated).astype(jnp.bfloat16)
        out_refs[d][row_count:] = extra_ref[d].astype(jnp.bfloat16)


def ready_kernel(proj_hbm, weight_hbm, table_ref, query_ref, weight_ref, proj_ref, sems):
    copies = [
        pltpu.make_async_copy(proj_hbm.at[0], proj_ref, sems.at[0]),
        pltpu.make_async_copy(weight_hbm, weight_ref, sems.at[1]),
    ]
    for copy in copies:
        copy.start()
    table = table_ref[0]
    group_count = table.shape[0]
    width = query_ref.shape[1] // group_count
    copies[0].wait()
    for g in range(group_count):
        lanes = slice(g * width, (g + 1) * width)
        query_ref[:, lanes] = short_sum(proj_ref[:, lanes].astype(jnp.float32), taps_of(table, g))
    copies[1].wait()


def filter_kernel(copies, lags, place_ref, table_ref, *refs):
    seq_count = (len(refs) - 2) * copies // (copies + 1)
    group_count = seq_count // copies
    in_refs, out_refs = refs[:seq_count], refs[seq_count : seq_count + group_count]
    gated_ref, extra_ref = refs[seq_count + group_count :]
    rows_sent, width = in_refs[0].shape
    row_count = rows_sent - EXTRA
    depth = REACH * row_count
    me = place_ref[0]
    group, part = me // copies, me % copies

    gated_ref[0:depth] = jnp.zeros((depth, width), jnp.bfloat16)
    for d in range(group_count):
        for x in range(copies):
            source = (group ^ d) * copies + (part ^ x)
            block = in_refs[x * group_count + d]
            base = pl.multiple_of(depth + source * row_count, row_count)
            gated_ref[pl.ds(base, row_count), :] = block[0:row_count]
            extra_ref[source] = block[row_count:].astype(jnp.float32)

    extras = [extra_ref[s] for s in range(seq_count)]
    lags_back = jnp.concatenate([e[0:1] for e in extras[::-1]], axis=0).astype(jnp.bfloat16)
    i = lax.broadcasted_iota(jnp.int32, (width, width), 0)
    k = lax.broadcasted_iota(jnp.int32, (width, width), 1)
    flip = jnp.where(i + k == lags - 1, 1.0, 0.0).astype(jnp.bfloat16)
    turned = jnp.dot(lags_back, flip, preferred_element_type=jnp.float32)
    span = depth + 2 * row_count
    first_lane = depth - lags * seq_count + 1
    blank = jnp.zeros((1, span - width), jnp.float32)
    line = jnp.zeros((1, span), jnp.float32)
    for s in range(seq_count):
        piece = jnp.concatenate([turned[s : s + 1], blank], axis=1)
        line = line + pltpu.roll(piece, first_lane + lags * s, axis=1)
    strip = pltpu.roll(
        jnp.broadcast_to(line, (row_count, span)), 0, axis=1, stride=1, stride_axis=0
    )
    strip = strip[:, : depth + row_count].astype(jnp.bfloat16)

    taps = [taps_of(table_ref[s], group) for s in (1, 2)]
    tile_rows = lax.broadcasted_iota(jnp.int32, (16, width), 0)
    before = jnp.zeros((EXTRA, width), jnp.float32)
    for s in range(seq_count):
        here = extras[s]
        base = depth + s * row_count
        tile = gated_ref[base : base + 16].astype(jnp.float32)
        heads = []
        for stream, head in enumerate((tile[0:2], here[1:3])):
            tap = taps[stream]
            first, second = head[0:1], head[1:2]
            older, newer = before[3 + 2 * stream : 4 + 2 * stream], before[4 + 2 * stream : 5 + 2 * stream]
            heads.append(
                (
                    tap[0] * first + tap[1] * newer + tap[2] * older,
                    tap[0] * second + tap[1] * first + tap[2] * newer,
                )
            )
        tile = jnp.where(tile_rows == 0, heads[0][0] * heads[1][0], tile)
        tile = jnp.where(tile_rows == 1, heads[0][1] * heads[1][1], tile)
        gated_ref[base : base + 16] = tile.astype(jnp.bfloat16)
        before = here

    for d in range(group_count):
        block = (group ^ d) * copies + part
        start = pl.multiple_of(block * row_count, row_count)
        source = gated_ref[pl.ds(start, depth + row_count), :]
        made = jnp.dot(strip, source, preferred_element_type=jnp.float32)
        out_refs[d][0:row_count] = made.astype(jnp.bfloat16)
        rim = jnp.where(block > 0, extra_ref[jnp.maximum(block - 1, 0), 8:], 0.0)
        out_refs[d][row_count:] = rim.astype(jnp.bfloat16)


def project_kernel(copies, seq_ref, place_ref, query_ref, table_ref, weight_ref, *refs):
    in_refs, (send_ref, keep_ref, mixed_ref) = refs[:-3], refs[-3:]
    row_count, width = in_refs[0].shape[0] - RIM, in_refs[0].shape[1]
    rows = lax.broadcasted_iota(jnp.int32, (8, width), 0)
    for d, long_ref in enumerate(in_refs):
        group = (seq_ref[0] // copies) ^ d
        lanes = pl.ds(pl.multiple_of(group * width, width), width)
        rim = long_ref[row_count:].astype(jnp.float32)
        older, newer = rim[0:1], rim[1:2]
        _, one, two = taps_of(table_ref[0], group)
        head = query_ref[0:8, lanes]
        head = head + jnp.where(rows == 0, one * newer + two * older, 0.0)
        head = head + jnp.where(rows == 1, two * newer, 0.0)
        query = jnp.concatenate([head, query_ref[8:, lanes]], axis=0)
        mixed_ref[:, lanes] = (query * long_ref[0:row_count].astype(jnp.float32)).astype(jnp.bfloat16)
    quarter = row_count // 4
    me = place_ref[0]

    def take(member):
        return mixed_ref[pl.ds(pl.multiple_of(member * quarter, quarter), quarter), :]

    ordered = jnp.concatenate([take(me ^ 1), take(me ^ 3), take(me), take(me ^ 2)], axis=0)
    step = 512
    for c in range(0, weight_ref.shape[1], step):
        made = jnp.dot(
            ordered, weight_ref[:, c : c + step], preferred_element_type=jnp.float32
        )
        send_ref[:, c : c + step] = made[: 2 * quarter].astype(jnp.bfloat16)
        keep_ref[:, c : c + step] = made[2 * quarter :]


def room(mib):
    return pltpu.CompilerParams(vmem_limit_bytes=mib << 20)


def cost(flops, moved):
    return pl.CostEstimate(flops=flops, bytes_accessed=moved, transcendentals=0)


def whole(space=pltpu.VMEM):
    return pl.BlockSpec(memory_space=space)


def in_hbm(array):
    return pltpu.with_memory_space_constraint(array, pltpu.HBM)


def swapped(array, axis, flip):
    return lax.ppermute(array, axis, [(i, i ^ flip) for i in range(lax.axis_size(axis))])


def exchange_form(projected, short_filter, long_filter, out_weight):
    row_count, _, chan_count = projected.shape
    group_count = short_filter.shape[1]
    width = chan_count // group_count
    out_count = out_weight.shape[1]
    seq_count = lax.axis_size("seq")
    copies = seq_count // group_count
    lags = long_filter.shape[1]
    rows_sent = row_count + EXTRA
    streams = in_hbm(jnp.transpose(projected, (1, 0, 2)))
    seq_place = lax.axis_index("seq").astype(jnp.int32).reshape(1)
    chan_place = lax.axis_index("chan").astype(jnp.int32).reshape(1)
    block_bytes = row_count * chan_count * 2

    *outgoing, table = pl.pallas_call(
        functools.partial(gate_kernel, copies),
        out_shape=[jax.ShapeDtypeStruct((rows_sent, width), jnp.bfloat16)] * group_count
        + [jax.ShapeDtypeStruct(short_filter.shape, jnp.float32)],
        in_specs=[whole(pltpu.SMEM)] + [whole(pltpu.HBM)] * 3,
        out_specs=[whole()] * (group_count + 1),
        scratch_shapes=[
            pltpu.VMEM((group_count, 2, row_count, width), projected.dtype),
            pltpu.VMEM(short_filter.shape, short_filter.dtype),
            pltpu.VMEM(long_filter.shape, long_filter.dtype),
            pltpu.VMEM((group_count, EXTRA, width), jnp.float32),
            pltpu.VMEM((8, chan_count), projected.dtype),
            pltpu.SemaphoreType.DMA((3 + group_count,)),
        ],
        compiler_params=room(4),
        cost_estimate=cost(12 * row_count * chan_count, 4 * block_bytes),
        name="gate",
    )(seq_place, streams, in_hbm(short_filter), in_hbm(long_filter))
    mine = list(outgoing)
    for d in range(group_count - 1, 0, -1):
        mine[d] = swapped(mine[d], "seq", d * copies)
    other = [swapped(block, "seq", 1) for block in mine]

    query, weight = pl.pallas_call(
        ready_kernel,
        out_shape=(
            jax.ShapeDtypeStruct((row_count, chan_count), jnp.float32),
            jax.ShapeDtypeStruct(out_weight.shape, out_weight.dtype),
        ),
        in_specs=[whole(pltpu.HBM)] * 2 + [whole()],
        out_specs=(whole(), whole()),
        scratch_shapes=[
            pltpu.VMEM((row_count, chan_count), projected.dtype),
            pltpu.SemaphoreType.DMA((2,)),
        ],
        compiler_params=room(4),
        cost_estimate=cost(6 * row_count * chan_count, 2 * chan_count * out_count + 3 * block_bytes),
        name="ready",
    )(streams, in_hbm(out_weight), table)

    made = pl.pallas_call(
        functools.partial(filter_kernel, copies, lags),
        out_shape=[jax.ShapeDtypeStruct((row_count + RIM, width), jnp.bfloat16)] * group_count,
        in_specs=[whole(pltpu.SMEM)] + [whole()] * (1 + seq_count),
        out_specs=[whole()] * group_count,
        scratch_shapes=[
            pltpu.VMEM(((REACH + seq_count) * row_count, width), jnp.bfloat16),
            pltpu.VMEM((seq_count, EXTRA, width), jnp.float32),
        ],
        compiler_params=room(4),
        cost_estimate=cost(
            2 * group_count * (REACH + 1) * row_count * row_count * width, 4 * block_bytes
        ),
        name="long_filter",
    )(seq_place, table, *mine, *other)
    returned = list(made)
    for d in range(group_count - 1, 0, -1):
        returned[d] = swapped(returned[d], "seq", d * copies)

    half = row_count // 2
    send, keep = pl.pallas_call(
        functools.partial(project_kernel, copies),
        out_shape=(
            jax.ShapeDtypeStruct((half, out_count), jnp.bfloat16),
            jax.ShapeDtypeStruct((half, out_count), jnp.float32),
        ),
        in_specs=[whole(pltpu.SMEM)] * 2 + [whole()] * (3 + group_count),
        out_specs=(whole(), whole()),
        scratch_shapes=[pltpu.VMEM((row_count, chan_count), jnp.bfloat16)],
        compiler_params=room(4),
        cost_estimate=cost(2 * row_count * chan_count * out_count, 2 * chan_count * out_count),
        name="project",
    )(seq_place, chan_place, query, table, weight, *returned)
    near = swapped(send, "chan", 1)
    quarter = half // 2
    onward = (keep[quarter:] + near[quarter:].astype(jnp.float32)).astype(jnp.bfloat16)
    far = swapped(onward, "chan", 2)
    kept = keep[:quarter] + near[:quarter].astype(jnp.float32)
    return (kept + far.astype(jnp.float32)).astype(jnp.bfloat16)


def on_device(projected, short_filter, long_filter, out_weight):
    row_count, _, chan_count = projected.shape
    group_count = short_filter.shape[1]
    width = chan_count // group_count
    seq_count = lax.axis_size("seq")
    exchanged = 3 * group_count * (row_count + EXTRA) * width
    ringed = REACH * row_count * chan_count
    fits = (
        seq_count == 2 * group_count
        and group_count in (2, 4, 8)
        and seq_count * long_filter.shape[1] <= REACH * row_count
        and long_filter.shape[1] <= width
        and width == 128
        and row_count % 64 == 0
        and short_filter.shape[-1] == 3
        and lax.axis_size("chan") == 4
    )
    form = exchange_form if fits and exchanged < ringed else ring_form
    return form(projected, short_filter, long_filter, out_weight)


def solution(mesh):
    return jax.shard_map(
        on_device,
        mesh=mesh,
        in_specs=(P("seq", None, "chan"), P(None, "chan", None), P("chan", "seq"), P("chan", None)),
        out_specs=P(("seq", "chan"), None),
        check_vma=False,
    )
```

```python
import functools

import jax
import jax.numpy as jnp
from jax import lax
from jax.experimental import pallas as pl
from jax.experimental.pallas import tpu as pltpu
from jax.sharding import PartitionSpec as P

REACH = 6
EXTRA = 16
RIM = 8


def shifted(array, axis, by):
    peers = lax.axis_size(axis)
    pairs = [(i, i + by) for i in range(peers) if 0 <= i + by < peers]
    return lax.ppermute(array, axis, pairs)


def toeplitz_block(padded, offset, row_count):
    group_count = padded.shape[0]
    window = lax.slice_in_dim(
        padded, offset * row_count + 1, offset * row_count + 2 * row_count, axis=1
    )
    tiled_rows = jnp.tile(window, (1, row_count + 1))[:, : 2 * row_count * row_count]
    tiled_rows = tiled_rows.reshape(group_count, row_count, 2 * row_count)
    return tiled_rows[:, :, :row_count][:, :, ::-1]


def ring_form(projected, short_filter, long_filter, out_weight):
    row_count, _, chan_count = projected.shape
    tap_count = short_filter.shape[-1]
    group_count = short_filter.shape[1]
    group_width = chan_count // group_count
    tail_rows = projected[row_count - tap_count + 1 :]
    arrived_rim = shifted(tail_rows, "seq", 1)
    padded_rows = jnp.concatenate([arrived_rim, projected], axis=0)
    channel_taps = jnp.repeat(short_filter.astype(jnp.float32), group_width, axis=1)
    streams = jnp.zeros((row_count, 3, chan_count), jnp.float32)
    for lag in range(tap_count):
        begin = tap_count - 1 - lag
        window = lax.slice_in_dim(padded_rows, begin, begin + row_count, axis=0)
        streams = streams + channel_taps[None, :, :, lag] * window.astype(jnp.float32)
    query_part = streams[:, 0]
    gated_input = (streams[:, 1] * streams[:, 2]).astype(jnp.bfloat16)
    filters = lax.all_gather(long_filter, "seq", axis=1, tiled=True)
    padded = jnp.pad(filters, ((0, 0), (row_count, row_count)))

    def add_offset(running, offset, source_block):
        matrix = toeplitz_block(padded, offset, row_count)
        shaped_block = source_block.reshape(row_count, group_count, group_width)
        return running + jnp.einsum(
            "gij,jgc->igc", matrix, shaped_block, preferred_element_type=jnp.float32
        )

    running = add_offset(
        jnp.zeros((row_count, group_count, group_width), jnp.float32), 0, gated_input
    )
    moving = gated_input
    for offset in range(1, REACH + 1):
        moving = shifted(moving, "seq", 1)
        running = add_offset(running, offset, moving)
    mixed_out = (query_part * running.reshape(row_count, chan_count)).astype(jnp.bfloat16)
    result = lax.psum_scatter(
        jnp.dot(mixed_out, out_weight, preferred_element_type=jnp.float32),
        "chan",
        scatter_dimension=0,
        tiled=True,
    )
    return result.astype(jnp.bfloat16)


def lagged(stream, lag):
    moved = pltpu.roll(stream, lag, axis=0)
    rows = lax.broadcasted_iota(jnp.int32, stream.shape, 0)
    return jnp.where(rows >= lag, moved, 0.0)


def taps_of(table, group):
    rows = lax.broadcasted_iota(jnp.int32, table.shape, 0)
    row = jnp.sum(jnp.where(rows == group, table, 0.0), axis=0, keepdims=True)
    return [row[:, m : m + 1] for m in range(3)]


def short_sum(stream, tap):
    return tap[0] * stream + tap[1] * lagged(stream, 1) + tap[2] * lagged(stream, 2)


def gate_kernel(place_ref, proj_hbm, short_hbm, long_hbm, *refs):
    group_count, row_count = long_hbm.shape[0], proj_hbm.shape[1]
    out_refs, table_ref = refs[:group_count], refs[group_count]
    proj_ref, short_ref, long_ref, extra_ref, tail_ref, sems = refs[group_count + 1 :]
    width = proj_ref.shape[-1]
    lags = long_ref.shape[1]
    mine = place_ref[0] % group_count
    small = [
        pltpu.make_async_copy(short_hbm, short_ref, sems.at[0]),
        pltpu.make_async_copy(long_hbm, long_ref, sems.at[1]),
        pltpu.make_async_copy(proj_hbm.at[0, row_count - 8 :], tail_ref, sems.at[2]),
    ]
    order = list(range(group_count))[::-1]
    large = {}
    for d in order:
        lanes = pl.ds(pl.multiple_of((mine ^ d) * width, width), width)
        large[d] = pltpu.make_async_copy(proj_hbm.at[1:3, :, lanes], proj_ref.at[d], sems.at[3 + d])
    for copy in small + [large[d] for d in order]:
        copy.start()
    extra_ref[...] = jnp.zeros_like(extra_ref)
    for copy in small:
        copy.wait()
    tables = [short_ref[s].astype(jnp.float32) for s in (1, 2)]
    for s in range(3):
        table_ref[s] = short_ref[s].astype(jnp.float32)
    long_rows = long_ref[...].astype(jnp.float32)
    long_row_ids = lax.broadcasted_iota(jnp.int32, long_rows.shape, 0)
    for d in order:
        group = mine ^ d
        taps = [taps_of(table, group) for table in tables]
        picked = jnp.where(long_row_ids == group, long_rows, 0.0)
        extra_ref[d, 0:1, 0:lags] = jnp.sum(picked, axis=0, keepdims=True)
        large[d].wait()
        key, value = (proj_ref[d, s].astype(jnp.float32) for s in range(2))
        gated = short_sum(key, taps[0]) * short_sum(value, taps[1])
        rows = lax.broadcasted_iota(jnp.int32, gated.shape, 0)
        extra_ref[d, 1:3] = value[0:2]
        extra_ref[d, 3:5] = key[row_count - 2 :]
        extra_ref[d, 5:7] = value[row_count - 2 :]
        lanes = pl.ds(pl.multiple_of(group * width, width), width)
        extra_ref[d, 8:10] = tail_ref[:, lanes].astype(jnp.float32)[6:8]
        out_refs[d][0:row_count] = jnp.where(rows < 2, key, gated).astype(jnp.bfloat16)
        out_refs[d][row_count:] = extra_ref[d].astype(jnp.bfloat16)


def ready_kernel(proj_hbm, weight_hbm, table_ref, query_ref, weight_ref, proj_ref, sems):
    copies = [
        pltpu.make_async_copy(proj_hbm.at[0], proj_ref, sems.at[0]),
        pltpu.make_async_copy(weight_hbm, weight_ref, sems.at[1]),
    ]
    for copy in copies:
        copy.start()
    table = table_ref[0]
    group_count = table.shape[0]
    width = query_ref.shape[1] // group_count
    copies[0].wait()
    for g in range(group_count):
        lanes = slice(g * width, (g + 1) * width)
        query_ref[:, lanes] = short_sum(proj_ref[:, lanes].astype(jnp.float32), taps_of(table, g))
    copies[1].wait()


def filter_kernel(copies, lags, place_ref, table_ref, *refs):
    seq_count = (len(refs) - 2) * copies // (copies + 1)
    group_count = seq_count // copies
    in_refs, out_refs = refs[:seq_count], refs[seq_count : seq_count + group_count]
    gated_ref, extra_ref = refs[seq_count + group_count :]
    rows_sent, width = in_refs[0].shape
    row_count = rows_sent - EXTRA
    depth = REACH * row_count
    me = place_ref[0]
    group, part = me % group_count, me // group_count

    gated_ref[0:depth] = jnp.zeros((depth, width), jnp.bfloat16)
    for d in range(group_count):
        for x in range(copies):
            source = (part ^ x) * group_count + (group ^ d)
            block = in_refs[x * group_count + d]
            base = pl.multiple_of(depth + source * row_count, row_count)
            gated_ref[pl.ds(base, row_count), :] = block[0:row_count]
            extra_ref[source] = block[row_count:].astype(jnp.float32)

    extras = [extra_ref[s] for s in range(seq_count)]
    lags_back = jnp.concatenate([e[0:1] for e in extras[::-1]], axis=0).astype(jnp.bfloat16)
    i = lax.broadcasted_iota(jnp.int32, (width, width), 0)
    k = lax.broadcasted_iota(jnp.int32, (width, width), 1)
    flip = jnp.where(i + k == lags - 1, 1.0, 0.0).astype(jnp.bfloat16)
    turned = jnp.dot(lags_back, flip, preferred_element_type=jnp.float32)
    span = depth + 2 * row_count
    first_lane = depth - lags * seq_count + 1
    blank = jnp.zeros((1, span - width), jnp.float32)
    line = jnp.zeros((1, span), jnp.float32)
    for s in range(seq_count):
        piece = jnp.concatenate([turned[s : s + 1], blank], axis=1)
        line = line + pltpu.roll(piece, first_lane + lags * s, axis=1)
    strip = pltpu.roll(
        jnp.broadcast_to(line, (row_count, span)), 0, axis=1, stride=1, stride_axis=0
    )
    strip = strip[:, : depth + row_count].astype(jnp.bfloat16)

    taps = [taps_of(table_ref[s], group) for s in (1, 2)]
    tile_rows = lax.broadcasted_iota(jnp.int32, (16, width), 0)
    before = jnp.zeros((EXTRA, width), jnp.float32)
    for s in range(seq_count):
        here = extras[s]
        base = depth + s * row_count
        tile = gated_ref[base : base + 16].astype(jnp.float32)
        heads = []
        for stream, head in enumerate((tile[0:2], here[1:3])):
            tap = taps[stream]
            first, second = head[0:1], head[1:2]
            older, newer = before[3 + 2 * stream : 4 + 2 * stream], before[4 + 2 * stream : 5 + 2 * stream]
            heads.append(
                (
                    tap[0] * first + tap[1] * newer + tap[2] * older,
                    tap[0] * second + tap[1] * first + tap[2] * newer,
                )
            )
        tile = jnp.where(tile_rows == 0, heads[0][0] * heads[1][0], tile)
        tile = jnp.where(tile_rows == 1, heads[0][1] * heads[1][1], tile)
        gated_ref[base : base + 16] = tile.astype(jnp.bfloat16)
        before = here

    for d in range(group_count):
        block = part * group_count + (group ^ d)
        start = pl.multiple_of(block * row_count, row_count)
        source = gated_ref[pl.ds(start, depth + row_count), :]
        made = jnp.dot(strip, source, preferred_element_type=jnp.float32)
        out_refs[d][0:row_count] = made.astype(jnp.bfloat16)
        rim = jnp.where(block > 0, extra_ref[jnp.maximum(block - 1, 0), 8:], 0.0)
        out_refs[d][row_count:] = rim.astype(jnp.bfloat16)


def project_kernel(seq_ref, place_ref, query_ref, table_ref, weight_ref, *refs):
    in_refs, (send_ref, keep_ref, mixed_ref) = refs[:-3], refs[-3:]
    row_count, width = in_refs[0].shape[0] - RIM, in_refs[0].shape[1]
    rows = lax.broadcasted_iota(jnp.int32, (8, width), 0)
    for d, long_ref in enumerate(in_refs):
        group = (seq_ref[0] % len(in_refs)) ^ d
        lanes = pl.ds(pl.multiple_of(group * width, width), width)
        rim = long_ref[row_count:].astype(jnp.float32)
        older, newer = rim[0:1], rim[1:2]
        _, one, two = taps_of(table_ref[0], group)
        head = query_ref[0:8, lanes]
        head = head + jnp.where(rows == 0, one * newer + two * older, 0.0)
        head = head + jnp.where(rows == 1, two * newer, 0.0)
        query = jnp.concatenate([head, query_ref[8:, lanes]], axis=0)
        mixed_ref[:, lanes] = (query * long_ref[0:row_count].astype(jnp.float32)).astype(jnp.bfloat16)
    quarter = row_count // 4
    me = place_ref[0]

    def take(member):
        return mixed_ref[pl.ds(pl.multiple_of(member * quarter, quarter), quarter), :]

    ordered = jnp.concatenate([take(me ^ 1), take(me ^ 3), take(me), take(me ^ 2)], axis=0)
    step = 512
    for c in range(0, weight_ref.shape[1], step):
        made = jnp.dot(
            ordered, weight_ref[:, c : c + step], preferred_element_type=jnp.float32
        )
        send_ref[:, c : c + step] = made[: 2 * quarter].astype(jnp.bfloat16)
        keep_ref[:, c : c + step] = made[2 * quarter :]


def room(mib):
    return pltpu.CompilerParams(vmem_limit_bytes=mib << 20)


def cost(flops, moved):
    return pl.CostEstimate(flops=flops, bytes_accessed=moved, transcendentals=0)


def whole(space=pltpu.VMEM):
    return pl.BlockSpec(memory_space=space)


def in_hbm(array):
    return pltpu.with_memory_space_constraint(array, pltpu.HBM)


def swapped(array, axis, flip):
    return lax.ppermute(array, axis, [(i, i ^ flip) for i in range(lax.axis_size(axis))])


def exchange_form(projected, short_filter, long_filter, out_weight):
    row_count, _, chan_count = projected.shape
    group_count = short_filter.shape[1]
    width = chan_count // group_count
    out_count = out_weight.shape[1]
    seq_count = lax.axis_size("seq")
    copies = seq_count // group_count
    lags = long_filter.shape[1]
    rows_sent = row_count + EXTRA
    streams = in_hbm(jnp.transpose(projected, (1, 0, 2)))
    seq_place = lax.axis_index("seq").astype(jnp.int32).reshape(1)
    chan_place = lax.axis_index("chan").astype(jnp.int32).reshape(1)
    block_bytes = row_count * chan_count * 2

    *outgoing, table = pl.pallas_call(
        gate_kernel,
        out_shape=[jax.ShapeDtypeStruct((rows_sent, width), jnp.bfloat16)] * group_count
        + [jax.ShapeDtypeStruct(short_filter.shape, jnp.float32)],
        in_specs=[whole(pltpu.SMEM)] + [whole(pltpu.HBM)] * 3,
        out_specs=[whole()] * (group_count + 1),
        scratch_shapes=[
            pltpu.VMEM((group_count, 2, row_count, width), projected.dtype),
            pltpu.VMEM(short_filter.shape, short_filter.dtype),
            pltpu.VMEM(long_filter.shape, long_filter.dtype),
            pltpu.VMEM((group_count, EXTRA, width), jnp.float32),
            pltpu.VMEM((8, chan_count), projected.dtype),
            pltpu.SemaphoreType.DMA((3 + group_count,)),
        ],
        compiler_params=room(4),
        cost_estimate=cost(12 * row_count * chan_count, 4 * block_bytes),
        name="gate",
    )(seq_place, streams, in_hbm(short_filter), in_hbm(long_filter))
    mine, other = list(outgoing), [None] * group_count
    for d in (1, 3, 2):
        mine[d] = swapped(mine[d], "seq", d)
    for pair in ((0, 1), (3, 2)):
        both = swapped(jnp.concatenate([mine[d] for d in pair]), "seq", group_count)
        for i, d in enumerate(pair):
            other[d] = both[i * rows_sent : (i + 1) * rows_sent]

    query, weight = pl.pallas_call(
        ready_kernel,
        out_shape=(
            jax.ShapeDtypeStruct((row_count, chan_count), jnp.float32),
            jax.ShapeDtypeStruct(out_weight.shape, out_weight.dtype),
        ),
        in_specs=[whole(pltpu.HBM)] * 2 + [whole()],
        out_specs=(whole(), whole()),
        scratch_shapes=[
            pltpu.VMEM((row_count, chan_count), projected.dtype),
            pltpu.SemaphoreType.DMA((2,)),
        ],
        compiler_params=room(4),
        cost_estimate=cost(6 * row_count * chan_count, 2 * chan_count * out_count + 3 * block_bytes),
        name="ready",
    )(streams, in_hbm(out_weight), table)

    made = pl.pallas_call(
        functools.partial(filter_kernel, copies, lags),
        out_shape=[jax.ShapeDtypeStruct((row_count + RIM, width), jnp.bfloat16)] * group_count,
        in_specs=[whole(pltpu.SMEM)] + [whole()] * (1 + seq_count),
        out_specs=[whole()] * group_count,
        scratch_shapes=[
            pltpu.VMEM(((REACH + seq_count) * row_count, width), jnp.bfloat16),
            pltpu.VMEM((seq_count, EXTRA, width), jnp.float32),
        ],
        compiler_params=room(4),
        cost_estimate=cost(
            2 * group_count * (REACH + 1) * row_count * row_count * width, 4 * block_bytes
        ),
        name="long_filter",
    )(seq_place, table, *mine, *other)
    returned = list(made)
    for d in (3, 2, 1):
        returned[d] = swapped(returned[d], "seq", d)

    half = row_count // 2
    send, keep = pl.pallas_call(
        project_kernel,
        out_shape=(
            jax.ShapeDtypeStruct((half, out_count), jnp.bfloat16),
            jax.ShapeDtypeStruct((half, out_count), jnp.float32),
        ),
        in_specs=[whole(pltpu.SMEM)] * 2 + [whole()] * (3 + group_count),
        out_specs=(whole(), whole()),
        scratch_shapes=[pltpu.VMEM((row_count, chan_count), jnp.bfloat16)],
        compiler_params=room(4),
        cost_estimate=cost(2 * row_count * chan_count * out_count, 2 * chan_count * out_count),
        name="project",
    )(seq_place, chan_place, query, table, weight, *returned)
    near = swapped(send, "chan", 1)
    quarter = half // 2
    onward = (keep[quarter:] + near[quarter:].astype(jnp.float32)).astype(jnp.bfloat16)
    far = swapped(onward, "chan", 2)
    kept = keep[:quarter] + near[:quarter].astype(jnp.float32)
    return (kept + far.astype(jnp.float32)).astype(jnp.bfloat16)


def on_device(projected, short_filter, long_filter, out_weight):
    row_count, _, chan_count = projected.shape
    group_count = short_filter.shape[1]
    width = chan_count // group_count
    seq_count = lax.axis_size("seq")
    exchanged = 3 * group_count * (row_count + EXTRA) * width
    ringed = REACH * row_count * chan_count
    fits = (
        seq_count == 2 * group_count
        and group_count == 4
        and seq_count * long_filter.shape[1] <= REACH * row_count
        and long_filter.shape[1] <= width
        and width == 128
        and row_count % 64 == 0
        and short_filter.shape[-1] == 3
        and lax.axis_size("chan") == 4
    )
    form = exchange_form if fits and exchanged < ringed else ring_form
    return form(projected, short_filter, long_filter, out_weight)


def solution(mesh):
    return jax.shard_map(
        on_device,
        mesh=mesh,
        in_specs=(P("seq", None, "chan"), P(None, "chan", None), P("chan", "seq"), P("chan", None)),
        out_specs=P(("seq", "chan"), None),
        check_vma=False,
    )
```
